32 devices in a mesh: section: 4 (over z), ep: 8 (over y, x, core).
Axes of the slice: x: 2, y: 2, z: 4, core: 2. Of those that a mesh axis runs over, the one named last changes fastest.
Arguments:
- flight_a: bfloat16 [4, 1024, 3584], P('section', 'ep'), may hold values from -6 to 6
- flight_b: bfloat16 [4, 1024, 3584], P('section', 'ep'), may hold values from -6 to 6
- routes_a: int32 [4, 1, 1024, 1], P('section', None, 'ep'), may hold values from 0 to 1; in each aligned block of 128 rows (0 to 127, 128 to 255, ..., all dimensions but the last counted through in order) at most 72 rows name the same one
- routes_b: int32 [4, 1, 1024, 1], P('section', None, 'ep'), may hold values from 0 to 1; in each aligned block of 128 rows (0 to 127, 128 to 255, ..., all dimensions but the last counted through in order) at most 72 rows name the same one
- scores_a: float32 [4, 1, 1024, 1], P('section', None, 'ep'), may hold values from 0.5 to 1.5
- scores_b: float32 [4, 1, 1024, 1], P('section', None, 'ep'), may hold values from 0.5 to 1.5
- norm_gain: float32 [4, 3584], P('section'), may hold values from 0.1 to 1.9
- w_gate: bfloat16 [4, 3584, 2048], P('section', None, 'ep'), may hold values from -0.09375 to 0.09375
- w_up: bfloat16 [4, 3584, 2048], P('section', None, 'ep'), may hold values from -0.09375 to 0.09375
- w_down: bfloat16 [4, 2048, 3584], P('section', 'ep'), may hold values from -0.1875 to 0.1875
Outputs:
- out_a: bfloat16 [4, 1024, 3584], P('section', 'ep')
- out_b: bfloat16 [4, 1024, 3584], P('section', 'ep')
The draws below stay inside these ranges and needn't reach their ends.
Inputs may be any that keep to these rules, and one draw needn't show every extreme that they name: `routes_a`: in each block of 128 rows that one device holds for one layer and step, no expert is named more than 72 times, a bound that some block reaches; a row never names one expert twice. `routes_b`: as for routes_a.
All inputs are finite; a program needn't handle non-finite values.
Results may differ from the reference program's by a relative error of at most 0.0054.
Values may be sent and summed in bfloat16 or wider, within the bound.
A program may use at most 128 MiB of HBM per device.

```python
import math
import jax
import jax.numpy as jnp
import numpy as np
from jax import lax

D = 3584
FFE = 1024
ES = 4
TOPK = 1
STEPS = 1
TOK_DEV = 128
EXPERTS = 2
CAP = 72
TOKENS = 1024
LAYERS = 4
N_EP = 8


def block_levels(stream_key, dims, split, smallest, largest):
    level, own = 1.0, jax.random.fold_in(stream_key, 6)
    for dim, parts in split:
        draws = jnp.exp(jax.random.uniform(jax.random.fold_in(own, dim), (parts,), jnp.float32, smallest / len(split), largest / len(split)))
        level = level * jnp.repeat(draws, dims[dim] // parts).reshape([-1 if axis == dim else 1 for axis in range(len(dims))])
    return level


def deal_out(rng, own, number, rows, number_of, top, most, skew):
    order = jax.random.permutation(rng, number_of)
    heavy_load, common = shares(number_of, rows * top, most, skew, True), shares(number_of, rows * top, most, skew, False)
    places = jnp.arange(number_of)

    def named(tallies, rotation):
        used = int((tallies > 0).sum())
        fixed = max(1, used // 4)
        passed = fixed + (places - fixed + rotation * (used - fixed)) % max(1, number_of - fixed)
        return jnp.zeros((number_of,), jnp.int32).at[order[jnp.where(places < fixed, places, passed)]].set(jnp.asarray(tallies, jnp.int32))

    tallies = jnp.where(number % 4 == 0, named(heavy_load, number // 4), named(common, number - number // 4 - 1))
    mixed = jax.random.permutation(jax.random.fold_in(own, 3), number_of)
    source_of, taker = mixed[0:number_of // 2 * 2:2], mixed[1:number_of // 2 * 2:2]
    margin = jnp.minimum(tallies[source_of] - 1, most - tallies[taker]) // 2
    margin = jnp.where((source_of == order[0]) | (taker == order[0]) | (tallies[taker] == 0), 0, jnp.maximum(margin, 0))
    passed = jax.random.randint(jax.random.fold_in(own, 4), (number_of // 2,), 0, 1 << 20) % (margin + 1)
    tallies = tallies.at[source_of].add(-passed).at[taker].add(passed)
    members = jnp.searchsorted(jnp.cumsum(tallies), jnp.arange(rows * top), side="right").astype(jnp.int32)
    listing = members.reshape(top, rows).T
    listing = listing[jax.random.permutation(jax.random.fold_in(own, 1), rows)]
    rotation = jax.random.randint(jax.random.fold_in(own, 2), (rows, 1), 0, top)
    return jnp.take_along_axis(listing, (jnp.arange(top)[None, :] + rotation) % top, axis=1)


def shares(count, total, bound, skew, full):
    portions = [(1 << 20) // math.isqrt(rank ** skew) + 1 for rank in range(1, count + 1)]
    largest = bound if full else min(bound, max(-(-total // count), total * portions[0] // sum(portions)))
    least = 1 if total - largest >= count - 1 else 0
    given, spare = [largest] + [least] * (count - 1), total - largest - least * (count - 1)
    while spare > 0:
        movable = [i for i in range(1, count) if given[i] < largest] or [i for i in range(1, count) if given[i] < bound]
        whole, budget = sum([portions[i] for i in movable]), spare
        for i in movable:
            extra = min(bound - given[i], max(1, budget * portions[i] // whole), spare)
            given[i] = given[i] + extra
            spare = spare - extra
    return np.array(given)


def normal_values(rng, dims, scale, most, cuts=(), kind=jnp.bfloat16):
    level = block_levels(rng, dims, cuts, -0.22, 0.18) if cuts else 1.0
    drawn = jax.random.normal(rng, dims, jnp.float32) * scale * level
    return jnp.minimum(jnp.maximum(drawn, -most), most).astype(kind)


def setup_inputs(seed: int = 0) -> dict:
    keys = jax.random.split(jax.random.key(seed), 11)
    flight_a = normal_values(keys[0], (LAYERS, TOKENS, D), 1.0, 6.0, ((0, 4), (1, 8)))
    flight_b = normal_values(keys[1], (LAYERS, TOKENS, D), 1.0, 6.0, ((0, 4), (1, 8)))
    routes_a_keys = jax.random.split(jax.random.fold_in(keys[2], 1), LAYERS * STEPS * TOKENS // TOK_DEV)
    routes_a_turns = jax.random.permutation(jax.random.fold_in(keys[2], 3), LAYERS * STEPS * TOKENS // TOK_DEV)
    routes_a = jax.vmap(lambda own, number: deal_out(jax.random.fold_in(keys[2], 2), own, number, TOK_DEV, EXPERTS, TOPK, CAP, 1))(routes_a_keys, routes_a_turns).reshape((LAYERS, STEPS, TOKENS, TOPK))
    routes_b_keys = jax.random.split(jax.random.fold_in(keys[3], 1), LAYERS * STEPS * TOKENS // TOK_DEV)
    routes_b_turns = jax.random.permutation(jax.random.fold_in(keys[3], 3), LAYERS * STEPS * TOKENS // TOK_DEV)
    routes_b = jax.vmap(lambda own, number: deal_out(jax.random.fold_in(keys[3], 2), own, number, TOK_DEV, EXPERTS, TOPK, CAP, 1))(routes_b_keys, routes_b_turns).reshape((LAYERS, STEPS, TOKENS, TOPK))
    scores_a = jnp.clip(0.5 + 1.0 * jax.random.uniform(keys[4], (LAYERS, STEPS, TOKENS, TOPK), jnp.float32) ** block_levels(keys[4], (LAYERS, STEPS, TOKENS, TOPK), ((0, 4), (2, 8)), -0.2, 0.2), 0.5, 1.5)
    scores_b = jnp.clip(0.5 + 1.0 * jax.random.uniform(keys[5], (LAYERS, STEPS, TOKENS, TOPK), jnp.float32) ** block_levels(keys[5], (LAYERS, STEPS, TOKENS, TOPK), ((0, 4), (2, 8)), -0.2, 0.2), 0.5, 1.5)
    norm_gain = jnp.clip(1.0 + 0.18 * jax.random.normal(keys[6], (LAYERS, D), jnp.float32), 0.1, 1.9)
    w_gate = normal_values(keys[7], (LAYERS, D, EXPERTS * FFE), D ** -0.5, 0.09375, ((0, 4), (2, 8)))
    w_up = normal_values(keys[8], (LAYERS, D, EXPERTS * FFE), D ** -0.5, 0.09375, ((0, 4), (2, 8)))
    w_down = normal_values(keys[9], (LAYERS, EXPERTS * FFE, D), FFE ** -0.5, 0.1875, ((0, 4), (1, 8)))
    return {"flight_a": flight_a, "flight_b": flight_b, "routes_a": routes_a, "routes_b": routes_b, "scores_a": scores_a, "scores_b": scores_b, "norm_gain": norm_gain, "w_gate": w_gate, "w_up": w_up, "w_down": w_down}


EPSILON = 1e-06

def rms_norm(current, gain):
    as_float = current.astype(jnp.float32)
    inverse_rms = lax.rsqrt(lax.optimization_barrier(jnp.mean(as_float * as_float, axis=-1, keepdims=True)) + EPSILON)
    return (as_float * inverse_rms * gain).astype(jnp.bfloat16)

def moe_layer(current, expert_ids, route_weights, gain, gate_rows, up_rows, down_rows):
    normed = rms_norm(current, gain)
    row_limit = N_EP * CAP
    slice_width = FFE // ES
    feature_width = current.shape[1]

    def add_expert(total_out, expert):
        chosen = expert_ids == expert
        coefficient = lax.optimization_barrier(jnp.sum(jnp.where(chosen, route_weights, 0.0), axis=1))
        routed = jnp.any(chosen, axis=1)
        token_index = jnp.nonzero(routed, size=row_limit, fill_value=0)[0].astype(jnp.int32)
        valid_rows = jnp.arange(row_limit, dtype=jnp.int32) < jnp.sum(routed.astype(jnp.int32))
        gathered = normed[token_index]
        gate_cols = lax.dynamic_slice_in_dim(gate_rows, expert * FFE, FFE, 1)
        up_cols = lax.dynamic_slice_in_dim(up_rows, expert * FFE, FFE, 1)
        down_part = lax.dynamic_slice_in_dim(down_rows, expert * FFE, FFE, 0)
        gate_act = jnp.dot(gathered, gate_cols, preferred_element_type=jnp.float32)
        up_act = jnp.dot(gathered, up_cols, preferred_element_type=jnp.float32)
        hidden = (jax.nn.silu(gate_act) * up_act).astype(jnp.bfloat16)
        summed = jnp.zeros((row_limit, feature_width), jnp.float32)
        for piece in range(ES):
            partial_value = jnp.dot(hidden[:, piece * slice_width:(piece + 1) * slice_width], down_part[piece * slice_width:(piece + 1) * slice_width], preferred_element_type=jnp.float32)
            rounded = lax.optimization_barrier(partial_value.astype(jnp.bfloat16))
            summed = summed + rounded.astype(jnp.float32)
        scale_rows = jnp.where(valid_rows, coefficient[token_index], 0.0)
        return (total_out.at[token_index].add(summed * scale_rows[:, None]), None)
    moe_out, _ = lax.scan(add_expert, jnp.zeros(current.shape, jnp.float32), jnp.arange(EXPERTS, dtype=jnp.int32))
    return (current.astype(jnp.float32) + moe_out).astype(jnp.bfloat16)

def reference(flight_a, flight_b, routes_a, routes_b, scores_a, scores_b, norm_gain, w_gate, w_up, w_down):
    results_a = [None] * LAYERS
    results_b = [None] * LAYERS
    for start_section in range(LAYERS):
        current = flight_a[start_section]
        for step_index in range(STEPS):
            layer_index = start_section + step_index
            if layer_index < LAYERS:
                current = moe_layer(current, routes_a[layer_index, step_index], scores_a[layer_index, step_index], norm_gain[layer_index], w_gate[layer_index], w_up[layer_index], w_down[layer_index])
        results_a[(start_section + STEPS) % LAYERS] = current
        current = flight_b[start_section]
        for step_index in range(STEPS):
            layer_index = start_section - step_index
            if layer_index >= 0:
                current = moe_layer(current, routes_b[layer_index, step_index], scores_b[layer_index, step_index], norm_gain[layer_index], w_gate[layer_index], w_up[layer_index], w_down[layer_index])
        results_b[(start_section - STEPS) % LAYERS] = current
    return (jnp.stack(results_a), jnp.stack(results_b))
```

```python
import functools

import jax
import jax.numpy as jnp
from jax import lax
from jax.experimental import pallas as pl
from jax.experimental.pallas import tpu as pltpu
from jax.sharding import PartitionSpec as P

ES = 4
TOPK = 1
CORES = 2
PAIR = ES // CORES

EPSILON = 1e-06
MESH = pl.DeviceIdType.MESH


def chunk_width(feature_width, most):
    return max(w for w in range(128, most + 1, 128) if feature_width % w == 0)


def window_kernel(
    ep_count,
    section_count,
    fa,
    fb,
    ra,
    rb,
    sa,
    sb,
    gain,
    w_gate,
    w_up,
    w_down,
    out_a,
    out_b,
    wg,
    wu,
    wd,
    own,
    there,
    leave,
    acc_g,
    acc_u,
    hid,
    part_out,
    part_in,
    home_out,
    home_in,
    final,
    w_sem,
    w_send,
    w_recv,
    a_send,
    a_recv,
    b_send,
    b_recv,
    c_send,
    c_recv,
    d_send,
    d_recv,
    e_send,
    e_recv,
    z_send,
    z_recv,
):
    groups = ep_count // ES
    chunks, rows, width = own.shape[1:]
    tok = fa.shape[0]
    both = 2 * tok
    sec = lax.axis_index("section")
    me = lax.axis_index("ep")
    group = me // ES
    pair = (me // CORES) % PAIR
    core = me % CORES

    def at(g, p, c):
        return (sec, g * ES + p * CORES + c)

    def group_at(i):
        return lax.rem(group + i, groups)

    partner = at(group, pair, 1 - core)
    across = at(group, 1 - pair, core)
    after = (lax.rem(sec + 1, section_count), me)
    before_dev = (lax.rem(sec + section_count - 1, section_count), me)

    loads = [
        pltpu.make_async_copy(src.at[0], dst.at[0], w_sem.at[n])
        for n, (src, dst) in enumerate(((w_gate, wg), (w_up, wu), (w_down, wd)))
    ]
    for load in loads:
        load.start()

    barrier = pltpu.get_barrier_semaphore()
    peers = [partner, across, after, before_dev]
    peers += [at(group_at(i), pair, core) for i in range(1, groups)]
    for peer in peers:
        pl.semaphore_signal(barrier, inc=1, device_id=peer, device_id_type=MESH)

    routes = jnp.concatenate([ra[...], rb[...]], axis=1)
    rel = routes - group
    rel = jnp.where(rel < 0, rel + groups, rel)
    padded = -(-groups // 8) * 8
    named = rel == lax.broadcasted_iota(jnp.int32, (padded, both), 0)
    named_f = jnp.where(named, 1.0, 0.0)
    first = lax.broadcasted_iota(jnp.int32, (both, both), 0)
    second = lax.broadcasted_iota(jnp.int32, (both, both), 1)
    earlier = jnp.where(first < second, 1.0, 0.0).astype(jnp.bfloat16)
    count = jnp.dot(named_f.astype(jnp.bfloat16), earlier, preferred_element_type=jnp.float32)
    slot = jnp.sum(count * named_f, axis=0, keepdims=True).astype(jnp.int32)
    place = rel * rows + slot
    diagonal = first == second
    place_col = jnp.sum(
        jnp.where(diagonal, place.astype(jnp.float32), 0.0), axis=1, keepdims=True
    ).astype(jnp.int32)
    scores = jnp.concatenate([sa[...], sb[...]], axis=1)
    score_col = jnp.sum(jnp.where(diagonal, scores, 0.0), axis=1, keepdims=True)
    pickers = [
        jnp.where(
            place == lax.broadcasted_iota(jnp.int32, (rows, both), 0) + i * rows, 1.0, 0.0
        ).astype(jnp.bfloat16)
        for i in range(groups)
    ]
    placers = [
        jnp.where(
            place_col == lax.broadcasted_iota(jnp.int32, (both, rows), 1) + i * rows, 1.0, 0.0
        ).astype(jnp.bfloat16)
        for i in range(groups)
    ]

    def inverse_rms(ref):
        def add(k, total):
            v = ref[:, pl.ds(pl.multiple_of(k * width, 128), width)].astype(jnp.float32)
            return total + jnp.sum(v * v, axis=1, keepdims=True)

        total = lax.fori_loop(0, chunks, add, jnp.zeros((tok, 1), jnp.float32))
        return lax.rsqrt(total / (chunks * width) + EPSILON)

    inv_a = inverse_rms(fa)
    inv_b = inverse_rms(fb)

    acc_g[...] = jnp.zeros_like(acc_g)
    acc_u[...] = jnp.zeros_like(acc_u)

    pl.semaphore_wait(barrier, len(peers))

    def remote(src, dst, send, recv, device):
        return pltpu.make_async_remote_copy(
            src_ref=src,
            dst_ref=dst,
            send_sem=send,
            recv_sem=recv,
            device_id=device,
            device_id_type=MESH,
        )

    def send_weights():
        return [
            remote(src.at[0], dst.at[1], w_send.at[n], w_recv.at[n], partner)
            for n, (src, dst) in enumerate(((w_gate, wg), (w_up, wu), (w_down, wd)))
        ]

    def own_rows(k):
        return remote(own.at[0, k], there.at[0, k], a_send.at[k], a_recv.at[k], across)

    def leaving(i, k):
        return remote(
            leave.at[i - 1, k],
            own.at[groups - i, k],
            b_send.at[i - 1, k],
            b_recv.at[groups - i - 1, k],
            at(group_at(i), pair, core),
        )

    def relay(j, k):
        return remote(
            own.at[j, k], there.at[j, k], c_send.at[j - 1, k], c_recv.at[j - 1, k], across
        )

    def part(j, k):
        return remote(part_out.at[j, k], part_in.at[j, k], d_send.at[j, k], d_recv.at[j, k], across)

    def homeward(j, k):
        return remote(
            home_out.at[j - 1, k],
            home_in.at[groups - j - 1, k],
            e_send.at[j - 1, k],
            e_recv.at[groups - j - 1, k],
            at(group_at(j), pair, core),
        )

    def lanes(k):
        return pl.ds(pl.multiple_of(k * width, 128), width)

    def result_a(k):
        return remote(final.at[0, k], out_a.at[:, lanes(k)], z_send.at[0, k], z_recv.at[0, k], after)

    def result_b(k):
        return remote(
            final.at[1, k], out_b.at[:, lanes(k)], z_send.at[1, k], z_recv.at[1, k], before_dev
        )

    def dispatch(k, _):
        scale = gain[:, lanes(k)]
        na = (fa[:, lanes(k)].astype(jnp.float32) * inv_a * scale).astype(jnp.bfloat16)
        nb = (fb[:, lanes(k)].astype(jnp.float32) * inv_b * scale).astype(jnp.bfloat16)
        normed = jnp.concatenate([na, nb], axis=0)
        for i in range(1, groups):
            leave[i - 1, k] = jnp.dot(
                pickers[i], normed, preferred_element_type=jnp.float32
            ).astype(jnp.bfloat16)
            leaving(i, k).start()
        own[0, k] = jnp.dot(pickers[0], normed, preferred_element_type=jnp.float32).astype(
            jnp.bfloat16
        )
        own_rows(k).start()
        return 0

    lax.fori_loop(0, chunks, dispatch, 0)
    for copy in send_weights():
        copy.start()
    for load in loads:
        load.wait()
    for copy in send_weights():
        copy.wait_recv()

    def project(side, buffer, j, k):
        block = buffer[j, k]
        for half in range(CORES):
            acc_g[side, j, half] += jnp.dot(
                block, wg[half, pl.ds(pl.multiple_of(k * width, 128), width), :],
                preferred_element_type=jnp.float32,
            )
            acc_u[side, j, half] += jnp.dot(
                block, wu[half, pl.ds(pl.multiple_of(k * width, 128), width), :],
                preferred_element_type=jnp.float32,
            )

    def activate(side, j):
        for half in range(CORES):
            g = acc_g[side, j, half]
            hid[side, j, half] = (g / (1.0 + jnp.exp(-g)) * acc_u[side, j, half]).astype(
                jnp.bfloat16
            )

    def down(side, j, k):
        total = jnp.dot(
            hid[side, j, 0], wd[0, :, lanes(k)], preferred_element_type=jnp.float32
        )
        for half in range(1, CORES):
            total += jnp.dot(
                hid[side, j, half], wd[half, :, lanes(k)], preferred_element_type=jnp.float32
            )
        return total

    def arrivals(k, _):
        for j in range(1, groups):
            leaving(groups - j, k).wait_recv()
            relay(j, k).start()
        for j in range(groups):
            project(0, own, j, k)
        return 0

    lax.fori_loop(0, chunks, arrivals, 0)
    for j in range(groups):
        activate(0, j)

    def from_across(k, _):
        own_rows(k).wait_recv()
        project(1, there, 0, k)
        return 0

    lax.fori_loop(0, chunks, from_across, 0)
    activate(1, 0)

    def send_part(j, k):
        part_out[j, k] = down(1, j, k).astype(jnp.bfloat16)
        part(j, k).start()

    send_part(0, 0)

    def from_relay(k, _):
        for j in range(1, groups):
            relay(j, k).wait_recv()
            project(1, there, j, k)
        return 0

    lax.fori_loop(0, chunks, from_relay, 0)
    for j in range(1, groups):
        activate(1, j)

    def send_parts(k, _):
        @pl.when(k > 0)
        def _():
            send_part(0, k)

        for j in range(1, groups):
            send_part(j, k)
        return 0

    lax.fori_loop(0, chunks, send_parts, 0)

    def finish(k):
        part(0, k).wait_recv()
        mine = (down(0, 0, k) + part_in[0, k].astype(jnp.float32)).astype(jnp.bfloat16)
        moe = jnp.dot(placers[0], mine, preferred_element_type=jnp.float32)
        for i in range(1, groups):
            homeward(groups - i, k).wait_recv()
            moe += jnp.dot(placers[i], home_in[i - 1, k], preferred_element_type=jnp.float32)
        moe = moe * score_col
        final[0, k] = (fa[:, lanes(k)].astype(jnp.float32) + moe[:tok]).astype(jnp.bfloat16)
        result_a(k).start()
        final[1, k] = (fb[:, lanes(k)].astype(jnp.float32) + moe[tok:]).astype(jnp.bfloat16)
        result_b(k).start()

    def returns(k, _):
        @pl.when(k < chunks)
        def _():
            for j in range(1, groups):
                part(j, k).wait_recv()
                home_out[j - 1, k] = (down(0, j, k) + part_in[j, k].astype(jnp.float32)).astype(
                    jnp.bfloat16
                )
                homeward(j, k).start()

        @pl.when(k > 0)
        def _():
            finish(k - 1)

        return 0

    lax.fori_loop(0, chunks + 1, returns, 0)

    for copy in send_weights():
        copy.wait_send()

    def drain(k, _):
        own_rows(k).wait_send()
        for i in range(1, groups):
            leaving(i, k).wait_send()
            relay(i, k).wait_send()
            homeward(i, k).wait_send()
        for j in range(groups):
            part(j, k).wait_send()
        result_a(k).wait()
        result_b(k).wait()
        return 0

    lax.fori_loop(0, chunks, drain, 0)


def on_device(
    flight_a, flight_b, routes_a, routes_b, scores_a, scores_b, norm_gain, w_gate, w_up, w_down
):
    ep_count = lax.axis_size("ep")
    section_count = lax.axis_size("section")
    groups = ep_count // ES
    tok, features = flight_a.shape[1:]
    hidden = w_gate.shape[2]
    capacity = min(tok, 9 * tok * TOPK * ES // (8 * ep_count))
    rows = -(-2 * capacity // 16) * 16
    width = chunk_width(features, 512)
    chunks = features // width
    bf16, f32 = jnp.bfloat16, jnp.float32
    others = groups - 1
    dma = pltpu.SemaphoreType.DMA
    vmem = pl.BlockSpec(memory_space=pltpu.VMEM)
    anywhere = pl.BlockSpec(memory_space=pl.ANY)
    out_a, out_b = pl.pallas_call(
        functools.partial(window_kernel, ep_count, section_count),
        out_shape=(
            jax.ShapeDtypeStruct((tok, features), bf16),
            jax.ShapeDtypeStruct((tok, features), bf16),
        ),
        in_specs=[vmem] * 7 + [anywhere] * 3,
        out_specs=(anywhere, anywhere),
        scratch_shapes=[
            pltpu.VMEM((CORES, features, hidden), bf16),
            pltpu.VMEM((CORES, features, hidden), bf16),
            pltpu.VMEM((CORES, hidden, features), bf16),
            pltpu.VMEM((groups, chunks, rows, width), bf16),
            pltpu.VMEM((groups, chunks, rows, width), bf16),
            pltpu.VMEM((others, chunks, rows, width), bf16),
            pltpu.VMEM((PAIR, groups, CORES, rows, hidden), f32),
            pltpu.VMEM((PAIR, groups, CORES, rows, hidden), f32),
            pltpu.VMEM((PAIR, groups, CORES, rows, hidden), bf16),
            pltpu.VMEM((groups, chunks, rows, width), bf16),
            pltpu.VMEM((groups, chunks, rows, width), bf16),
            pltpu.VMEM((others, chunks, rows, width), bf16),
            pltpu.VMEM((others, chunks, rows, width), bf16),
            pltpu.VMEM((2, chunks, tok, width), bf16),
            dma((3,)),
            dma((3,)),
            dma((3,)),
            dma((chunks,)),
            dma((chunks,)),
            dma((others, chunks)),
            dma((others, chunks)),
            dma((others, chunks)),
            dma((others, chunks)),
            dma((groups, chunks)),
            dma((groups, chunks)),
            dma((others, chunks)),
            dma((others, chunks)),
            dma((2, chunks)),
            dma((2, chunks)),
        ],
        compiler_params=pltpu.CompilerParams(
            collective_id=0, has_side_effects=True, vmem_limit_bytes=60 * 1024 * 1024
        ),
    )(
        flight_a[0],
        flight_b[0],
        routes_a.reshape(1, tok),
        routes_b.reshape(1, tok),
        scores_a.reshape(1, tok),
        scores_b.reshape(1, tok),
        norm_gain,
        w_gate,
        w_up,
        w_down,
    )
    return (out_a[None], out_b[None])


def solution(mesh):
    placed = (
        P("section", "ep", None),
        P("section", "ep", None),
        P("section", None, "ep", None),
        P("section", None, "ep", None),
        P("section", None, "ep", None),
        P("section", None, "ep", None),
        P("section", None),
        P("section", None, "ep"),
        P("section", None, "ep"),
        P("section", "ep", None),
    )
    return jax.shard_map(
        on_device,
        mesh=mesh,
        in_specs=placed,
        out_specs=(P("section", "ep", None), P("section", "ep", None)),
        check_vma=False,
    )
```

```python
import functools

import jax
import jax.numpy as jnp
from jax import lax
from jax.experimental import pallas as pl
from jax.experimental.pallas import tpu as pltpu
from jax.sharding import PartitionSpec as P

ES = 4
TOPK = 1
CORES = 2
PAIR = ES // CORES

EPSILON = 1e-06
MESH = pl.DeviceIdType.MESH


def chunk_width(feature_width, most):
    return max(w for w in range(128, most + 1, 128) if feature_width % w == 0)


def window_kernel(
    ep_count,
    section_count,
    fa,
    fb,
    ra,
    rb,
    sa,
    sb,
    gain,
    w_gate,
    w_up,
    w_down,
    out_a,
    out_b,
    wg,
    wu,
    wd,
    own,
    there,
    leave,
    acc_g,
    acc_u,
    hid,
    part_out,
    part_in,
    home_out,
    home_in,
    final,
    w_sem,
    w_send,
    w_recv,
    a_send,
    a_recv,
    b_send,
    b_recv,
    c_send,
    c_recv,
    d_send,
    d_recv,
    e_send,
    e_recv,
    z_send,
    z_recv,
):
    groups = ep_count // ES
    chunks, rows, width = own.shape[1:]
    tok = fa.shape[0]
    both = 2 * tok
    ahead = min(2, chunks)
    sec = lax.axis_index("section")
    me = lax.axis_index("ep")
    group = me // ES
    pair = (me // CORES) % PAIR
    core = me % CORES

    def at(g, p, c):
        return (sec, g * ES + p * CORES + c)

    def group_at(i):
        return lax.rem(group + i, groups)

    partner = at(group, pair, 1 - core)
    across = at(group, 1 - pair, core)
    after = (lax.rem(sec + 1, section_count), me)
    before_dev = (lax.rem(sec + section_count - 1, section_count), me)

    loads = [
        pltpu.make_async_copy(src.at[0], dst.at[0], w_sem.at[n])
        for n, (src, dst) in enumerate(((w_gate, wg), (w_up, wu), (w_down, wd)))
    ]
    for load in loads:
        load.start()

    barrier = pltpu.get_barrier_semaphore()
    peers = [partner, across, after, before_dev]
    peers += [at(group_at(i), pair, core) for i in range(1, groups)]
    for peer in peers:
        pl.semaphore_signal(barrier, inc=1, device_id=peer, device_id_type=MESH)

    routes = jnp.concatenate([ra[...], rb[...]], axis=1)
    rel = routes - group
    rel = jnp.where(rel < 0, rel + groups, rel)
    padded = -(-groups // 8) * 8
    named = rel == lax.broadcasted_iota(jnp.int32, (padded, both), 0)
    named_f = jnp.where(named, 1.0, 0.0)
    first = lax.broadcasted_iota(jnp.int32, (both, both), 0)
    second = lax.broadcasted_iota(jnp.int32, (both, both), 1)
    earlier = jnp.where(first < second, 1.0, 0.0).astype(jnp.bfloat16)
    count = jnp.dot(named_f.astype(jnp.bfloat16), earlier, preferred_element_type=jnp.float32)
    slot = jnp.sum(count * named_f, axis=0, keepdims=True).astype(jnp.int32)
    place = rel * rows + slot
    diagonal = first == second
    place_col = jnp.sum(
        jnp.where(diagonal, place.astype(jnp.float32), 0.0), axis=1, keepdims=True
    ).astype(jnp.int32)
    scores = jnp.concatenate([sa[...], sb[...]], axis=1)
    score_col = jnp.sum(jnp.where(diagonal, scores, 0.0), axis=1, keepdims=True)
    pickers = [
        jnp.where(
            place == lax.broadcasted_iota(jnp.int32, (rows, both), 0) + i * rows, 1.0, 0.0
        ).astype(jnp.bfloat16)
        for i in range(groups)
    ]
    placers = [
        jnp.where(
            place_col == lax.broadcasted_iota(jnp.int32, (both, rows), 1) + i * rows, 1.0, 0.0
        ).astype(jnp.bfloat16)
        for i in range(groups)
    ]

    def inverse_rms(ref):
        def add(k, total):
            v = ref[:, pl.ds(pl.multiple_of(k * width, 128), width)].astype(jnp.float32)
            return total + jnp.sum(v * v, axis=1, keepdims=True)

        total = lax.fori_loop(0, chunks, add, jnp.zeros((tok, 1), jnp.float32))
        return lax.rsqrt(total / (chunks * width) + EPSILON)

    inv_a = inverse_rms(fa)
    inv_b = inverse_rms(fb)

    acc_g[...] = jnp.zeros_like(acc_g)
    acc_u[...] = jnp.zeros_like(acc_u)

    pl.semaphore_wait(barrier, len(peers))

    def remote(src, dst, send, recv, device):
        return pltpu.make_async_remote_copy(
            src_ref=src,
            dst_ref=dst,
            send_sem=send,
            recv_sem=recv,
            device_id=device,
            device_id_type=MESH,
        )

    def send_weights():
        return [
            remote(src.at[0], dst.at[1], w_send.at[n], w_recv.at[n], partner)
            for n, (src, dst) in enumerate(((w_gate, wg), (w_up, wu), (w_down, wd)))
        ]

    def own_rows(k):
        return remote(own.at[0, k], there.at[0, k], a_send.at[k], a_recv.at[k], across)

    def leaving(i, k):
        return remote(
            leave.at[i - 1, k],
            own.at[groups - i, k],
            b_send.at[i - 1, k],
            b_recv.at[groups - i - 1, k],
            at(group_at(i), pair, core),
        )

    def relay(j, k):
        return remote(
            own.at[j, k], there.at[j, k], c_send.at[j - 1, k], c_recv.at[j - 1, k], across
        )

    def part(j, k):
        return remote(part_out.at[j, k], part_in.at[j, k], d_send.at[j, k], d_recv.at[j, k], across)

    def homeward(j, k):
        return remote(
            home_out.at[j - 1, k],
            home_in.at[groups - j - 1, k],
            e_send.at[j - 1, k],
            e_recv.at[groups - j - 1, k],
            at(group_at(j), pair, core),
        )

    def lanes(k):
        return pl.ds(pl.multiple_of(k * width, 128), width)

    def result_a(k):
        return remote(final.at[0, k], out_a.at[:, lanes(k)], z_send.at[0, k], z_recv.at[0, k], after)

    def result_b(k):
        return remote(
            final.at[1, k], out_b.at[:, lanes(k)], z_send.at[1, k], z_recv.at[1, k], before_dev
        )

    def dispatch(k, _):
        scale = gain[:, lanes(k)]
        na = (fa[:, lanes(k)].astype(jnp.float32) * inv_a * scale).astype(jnp.bfloat16)
        nb = (fb[:, lanes(k)].astype(jnp.float32) * inv_b * scale).astype(jnp.bfloat16)
        normed = jnp.concatenate([na, nb], axis=0)
        for i in range(1, groups):
            leave[i - 1, k] = jnp.dot(
                pickers[i], normed, preferred_element_type=jnp.float32
            ).astype(jnp.bfloat16)
            leaving(i, k).start()
        own[0, k] = jnp.dot(pickers[0], normed, preferred_element_type=jnp.float32).astype(
            jnp.bfloat16
        )
        own_rows(k).start()
        return 0

    lax.fori_loop(0, chunks, dispatch, 0)
    for copy in send_weights():
        copy.start()
    for load in loads:
        load.wait()
    for copy in send_weights():
        copy.wait_recv()

    def project(side, buffer, j, k):
        block = buffer[j, k]
        for half in range(CORES):
            acc_g[side, j, half] += jnp.dot(
                block, wg[half, pl.ds(pl.multiple_of(k * width, 128), width), :],
                preferred_element_type=jnp.float32,
            )
            acc_u[side, j, half] += jnp.dot(
                block, wu[half, pl.ds(pl.multiple_of(k * width, 128), width), :],
                preferred_element_type=jnp.float32,
            )

    def activate(side, j):
        for half in range(CORES):
            g = acc_g[side, j, half]
            hid[side, j, half] = (g / (1.0 + jnp.exp(-g)) * acc_u[side, j, half]).astype(
                jnp.bfloat16
            )

    def down(side, j, k):
        total = jnp.dot(
            hid[side, j, 0], wd[0, :, lanes(k)], preferred_element_type=jnp.float32
        )
        for half in range(1, CORES):
            total += jnp.dot(
                hid[side, j, half], wd[half, :, lanes(k)], preferred_element_type=jnp.float32
            )
        return total

    def arrivals(k, _):
        for j in range(1, groups):
            leaving(groups - j, k).wait_recv()
            relay(j, k).start()
        for j in range(groups):
            project(0, own, j, k)
        return 0

    lax.fori_loop(0, chunks, arrivals, 0)
    for j in range(groups):
        activate(0, j)

    def from_across(k, _):
        own_rows(k).wait_recv()
        project(1, there, 0, k)
        return 0

    lax.fori_loop(0, chunks, from_across, 0)
    activate(1, 0)

    def send_part(j, k):
        part_out[j, k] = down(1, j, k).astype(jnp.bfloat16)
        part(j, k).start()

    lax.fori_loop(0, ahead, lambda k, _: send_part(0, k) or 0, 0)

    def from_relay(k, _):
        for j in range(1, groups):
            relay(j, k).wait_recv()
            project(1, there, j, k)
        return 0

    lax.fori_loop(0, chunks, from_relay, 0)
    for j in range(1, groups):
        activate(1, j)

    def send_parts(k, _):
        for j in range(1, groups):
            send_part(j, k)

        @pl.when(k >= ahead)
        def _():
            send_part(0, k)

        return 0

    lax.fori_loop(0, chunks, send_parts, 0)

    def finish(k):
        part(0, k).wait_recv()
        mine = (down(0, 0, k) + part_in[0, k].astype(jnp.float32)).astype(jnp.bfloat16)
        moe = jnp.dot(placers[0], mine, preferred_element_type=jnp.float32)
        for i in range(1, groups):
            homeward(groups - i, k).wait_recv()
            moe += jnp.dot(placers[i], home_in[i - 1, k], preferred_element_type=jnp.float32)
        moe = moe * score_col
        final[0, k] = (fa[:, lanes(k)].astype(jnp.float32) + moe[:tok]).astype(jnp.bfloat16)
        result_a(k).start()
        final[1, k] = (fb[:, lanes(k)].astype(jnp.float32) + moe[tok:]).astype(jnp.bfloat16)
        result_b(k).start()

    def returns(k, _):
        @pl.when(k < chunks)
        def _():
            for j in range(1, groups):
                part(j, k).wait_recv()
                home_out[j - 1, k] = (down(0, j, k) + part_in[j, k].astype(jnp.float32)).astype(
                    jnp.bfloat16
                )
                homeward(j, k).start()

        @pl.when(k > 0)
        def _():
            finish(k - 1)

        return 0

    lax.fori_loop(0, chunks + 1, returns, 0)

    for copy in send_weights():
        copy.wait_send()

    def drain(k, _):
        own_rows(k).wait_send()
        for i in range(1, groups):
            leaving(i, k).wait_send()
            relay(i, k).wait_send()
            homeward(i, k).wait_send()
        for j in range(groups):
            part(j, k).wait_send()
        result_a(k).wait()
        result_b(k).wait()
        return 0

    lax.fori_loop(0, chunks, drain, 0)


def on_device(
    flight_a, flight_b, routes_a, routes_b, scores_a, scores_b, norm_gain, w_gate, w_up, w_down
):
    ep_count = lax.axis_size("ep")
    section_count = lax.axis_size("section")
    groups = ep_count // ES
    tok, features = flight_a.shape[1:]
    hidden = w_gate.shape[2]
    capacity = min(tok, 9 * tok * TOPK * ES // (8 * ep_count))
    rows = -(-2 * capacity // 16) * 16
    width = chunk_width(features, 256)
    chunks = features // width
    bf16, f32 = jnp.bfloat16, jnp.float32
    others = groups - 1
    dma = pltpu.SemaphoreType.DMA
    vmem = pl.BlockSpec(memory_space=pltpu.VMEM)
    anywhere = pl.BlockSpec(memory_space=pl.ANY)
    out_a, out_b = pl.pallas_call(
        functools.partial(window_kernel, ep_count, section_count),
        out_shape=(
            pltpu.VMEM((tok, features), bf16),
            pltpu.VMEM((tok, features), bf16),
        ),
        in_specs=[vmem] * 7 + [anywhere] * 3,
        out_specs=(vmem, vmem),
        scratch_shapes=[
            pltpu.VMEM((CORES, features, hidden), bf16),
            pltpu.VMEM((CORES, features, hidden), bf16),
            pltpu.VMEM((CORES, hidden, features), bf16),
            pltpu.VMEM((groups, chunks, rows, width), bf16),
            pltpu.VMEM((groups, chunks, rows, width), bf16),
            pltpu.VMEM((others, chunks, rows, width), bf16),
            pltpu.VMEM((PAIR, groups, CORES, rows, hidden), f32),
            pltpu.VMEM((PAIR, groups, CORES, rows, hidden), f32),
            pltpu.VMEM((PAIR, groups, CORES, rows, hidden), bf16),
            pltpu.VMEM((groups, chunks, rows, width), bf16),
            pltpu.VMEM((groups, chunks, rows, width), bf16),
            pltpu.VMEM((others, chunks, rows, width), bf16),
            pltpu.VMEM((others, chunks, rows, width), bf16),
            pltpu.VMEM((2, chunks, tok, width), bf16),
            dma((3,)),
            dma((3,)),
            dma((3,)),
            dma((chunks,)),
            dma((chunks,)),
            dma((others, chunks)),
            dma((others, chunks)),
            dma((others, chunks)),
            dma((others, chunks)),
            dma((groups, chunks)),
            dma((groups, chunks)),
            dma((others, chunks)),
            dma((others, chunks)),
            dma((2, chunks)),
            dma((2, chunks)),
        ],
        compiler_params=pltpu.CompilerParams(
            collective_id=0, has_side_effects=True, vmem_limit_bytes=60 * 1024 * 1024
        ),
    )(
        flight_a[0],
        flight_b[0],
        routes_a.reshape(1, tok),
        routes_b.reshape(1, tok),
        scores_a.reshape(1, tok),
        scores_b.reshape(1, tok),
        norm_gain,
        w_gate,
        w_up,
        w_down,
    )
    return (out_a[None], out_b[None])


def solution(mesh):
    placed = (
        P("section", "ep", None),
        P("section", "ep", None),
        P("section", None, "ep", None),
        P("section", None, "ep", None),
        P("section", None, "ep", None),
        P("section", None, "ep", None),
        P("section", None),
        P("section", None, "ep"),
        P("section", None, "ep"),
        P("section", "ep", None),
    )
    return jax.shard_map(
        on_device,
        mesh=mesh,
        in_specs=placed,
        out_specs=(P("section", "ep", None), P("section", "ep", None)),
        check_vma=False,
    )
```

```python
import functools

import jax
import jax.numpy as jnp
from jax import lax
from jax.experimental import pallas as pl
from jax.experimental.pallas import tpu as pltpu
from jax.sharding import PartitionSpec as P

ES = 4
TOPK = 1
CORES = 2
PAIR = ES // CORES

EPSILON = 1e-06
MESH = pl.DeviceIdType.MESH


def chunk_width(feature_width, most):
    return max(w for w in range(128, most + 1, 128) if feature_width % w == 0)


def spread_chunks(groups, chunks, rows, both):
    def longest(n):
        across = n * both + (chunks - n) * groups * rows
        between = (groups - 1) * rows * (chunks + n)
        return max(across, between), n

    return min(longest(n) for n in range(chunks + 1))[1]


def window_kernel(
    ep_count,
    section_count,
    fa,
    fb,
    ra,
    rb,
    sa,
    sb,
    gain,
    w_gate,
    w_up,
    w_down,
    out_a,
    out_b,
    wg,
    wu,
    wd,
    own,
    there,
    leave,
    raw_out,
    raw_in,
    passed,
    place_out,
    place_in,
    acc_g,
    acc_u,
    hid,
    part_out,
    part_in,
    home_out,
    home_in,
    final,
    w_sem,
    p_send,
    p_recv,
    w_send,
    w_recv,
    a_send,
    a_recv,
    b_send,
    b_recv,
    c_send,
    c_recv,
    d_send,
    d_recv,
    e_send,
    e_recv,
    z_send,
    z_recv,
):
    groups = ep_count // ES
    chunks, rows, width = own.shape[1:]
    tok = fa.shape[0]
    both = 2 * tok
    ahead = min(2, chunks)
    spread = spread_chunks(groups, chunks, rows, both)
    sec = lax.axis_index("section")
    me = lax.axis_index("ep")
    group = me // ES
    pair = (me // CORES) % PAIR
    core = me % CORES

    def at(g, p, c):
        return (sec, g * ES + p * CORES + c)

    def group_at(i):
        return lax.rem(group + i, groups)

    partner = at(group, pair, 1 - core)
    across = at(group, 1 - pair, core)
    after = (lax.rem(sec + 1, section_count), me)
    before_dev = (lax.rem(sec + section_count - 1, section_count), me)

    loads = [
        pltpu.make_async_copy(src.at[0], dst.at[0], w_sem.at[n])
        for n, (src, dst) in enumerate(((w_gate, wg), (w_up, wu), (w_down, wd)))
    ]
    for load in loads:
        load.start()

    barrier = pltpu.get_barrier_semaphore()
    peers = [partner, across, after, before_dev]
    peers += [at(group_at(i), pair, core) for i in range(1, groups)]
    for peer in peers:
        pl.semaphore_signal(barrier, inc=1, device_id=peer, device_id_type=MESH)

    routes = jnp.concatenate([ra[...], rb[...]], axis=1)
    rel = routes - group
    rel = jnp.where(rel < 0, rel + groups, rel)
    padded = -(-groups // 8) * 8
    named = rel == lax.broadcasted_iota(jnp.int32, (padded, both), 0)
    named_f = jnp.where(named, 1.0, 0.0)
    first = lax.broadcasted_iota(jnp.int32, (both, both), 0)
    second = lax.broadcasted_iota(jnp.int32, (both, both), 1)
    earlier = jnp.where(first < second, 1.0, 0.0).astype(jnp.bfloat16)
    count = jnp.dot(named_f.astype(jnp.bfloat16), earlier, preferred_element_type=jnp.float32)
    slot = jnp.sum(count * named_f, axis=0, keepdims=True).astype(jnp.int32)
    place = rel * rows + slot
    diagonal = first == second
    place_col = jnp.sum(
        jnp.where(diagonal, place.astype(jnp.float32), 0.0), axis=1, keepdims=True
    ).astype(jnp.int32)
    scores = jnp.concatenate([sa[...], sb[...]], axis=1)
    score_col = jnp.sum(jnp.where(diagonal, scores, 0.0), axis=1, keepdims=True)
    place_out[...] = place

    def pick(places):
        return [
            jnp.where(
                places == lax.broadcasted_iota(jnp.int32, (rows, both), 0) + i * rows, 1.0, 0.0
            ).astype(jnp.bfloat16)
            for i in range(groups)
        ]

    pickers = pick(place)
    placers = [
        jnp.where(
            place_col == lax.broadcasted_iota(jnp.int32, (both, rows), 1) + i * rows, 1.0, 0.0
        ).astype(jnp.bfloat16)
        for i in range(groups)
    ]

    def inverse_rms(ref):
        def add(k, total):
            v = ref[:, pl.ds(pl.multiple_of(k * width, 128), width)].astype(jnp.float32)
            return total + jnp.sum(v * v, axis=1, keepdims=True)

        total = lax.fori_loop(0, chunks, add, jnp.zeros((tok, 1), jnp.float32))
        return lax.rsqrt(total / (chunks * width) + EPSILON)

    inv_a = inverse_rms(fa)
    inv_b = inverse_rms(fb)

    acc_g[...] = jnp.zeros_like(acc_g)
    acc_u[...] = jnp.zeros_like(acc_u)

    pl.semaphore_wait(barrier, len(peers))

    def remote(src, dst, send, recv, device):
        return pltpu.make_async_remote_copy(
            src_ref=src,
            dst_ref=dst,
            send_sem=send,
            recv_sem=recv,
            device_id=device,
            device_id_type=MESH,
        )

    def send_weights():
        return [
            remote(src.at[0], dst.at[1], w_send.at[n], w_recv.at[n], partner)
            for n, (src, dst) in enumerate(((w_gate, wg), (w_up, wu), (w_down, wd)))
        ]

    def own_rows(k):
        return remote(own.at[0, k], there.at[0, k], a_send.at[k], a_recv.at[k], across)

    def places():
        return remote(place_out, place_in, p_send.at[0], p_recv.at[0], across)

    def raw_rows(k):
        return remote(raw_out.at[k], raw_in.at[k], a_send.at[k], a_recv.at[k], across)

    def passing(i, k):
        return remote(
            passed.at[i - 1, k],
            there.at[groups - i, k],
            c_send.at[i - 1, k],
            c_recv.at[groups - i - 1, k],
            at(group_at(i), pair, core),
        )

    def leaving(i, k):
        return remote(
            leave.at[i - 1, k],
            own.at[groups - i, k],
            b_send.at[i - 1, k],
            b_recv.at[groups - i - 1, k],
            at(group_at(i), pair, core),
        )

    def relay(j, k):
        return remote(
            own.at[j, k], there.at[j, k], c_send.at[j - 1, k], c_recv.at[j - 1, k], across
        )

    def part(j, k):
        return remote(part_out.at[j, k], part_in.at[j, k], d_send.at[j, k], d_recv.at[j, k], across)

    def homeward(j, k):
        return remote(
            home_out.at[j - 1, k],
            home_in.at[groups - j - 1, k],
            e_send.at[j - 1, k],
            e_recv.at[groups - j - 1, k],
            at(group_at(j), pair, core),
        )

    def lanes(k):
        return pl.ds(pl.multiple_of(k * width, 128), width)

    def result_a(k):
        return remote(final.at[0, k], out_a.at[:, lanes(k)], z_send.at[0, k], z_recv.at[0, k], after)

    def result_b(k):
        return remote(
            final.at[1, k], out_b.at[:, lanes(k)], z_send.at[1, k], z_recv.at[1, k], before_dev
        )

    def dispatch(k, _):
        scale = gain[:, lanes(k)]
        na = (fa[:, lanes(k)].astype(jnp.float32) * inv_a * scale).astype(jnp.bfloat16)
        nb = (fb[:, lanes(k)].astype(jnp.float32) * inv_b * scale).astype(jnp.bfloat16)
        normed = jnp.concatenate([na, nb], axis=0)

        @pl.when(k < spread)
        def _():
            raw_out[k] = normed
            raw_rows(k).start()

        for i in range(1, groups):
            leave[i - 1, k] = jnp.dot(
                pickers[i], normed, preferred_element_type=jnp.float32
            ).astype(jnp.bfloat16)
            leaving(i, k).start()
        own[0, k] = jnp.dot(pickers[0], normed, preferred_element_type=jnp.float32).astype(
            jnp.bfloat16
        )

        @pl.when(k >= spread)
        def _():
            own_rows(k).start()

        return 0

    places().start()
    lax.fori_loop(0, chunks, dispatch, 0)
    for copy in send_weights():
        copy.start()
    for load in loads:
        load.wait()
    places().wait_recv()
    pair_pickers = pick(place_in[...])
    for copy in send_weights():
        copy.wait_recv()

    def project(side, buffer, j, k):
        block = buffer[j, k]
        for half in range(CORES):
            acc_g[side, j, half] += jnp.dot(
                block, wg[half, pl.ds(pl.multiple_of(k * width, 128), width), :],
                preferred_element_type=jnp.float32,
            )
            acc_u[side, j, half] += jnp.dot(
                block, wu[half, pl.ds(pl.multiple_of(k * width, 128), width), :],
                preferred_element_type=jnp.float32,
            )

    def activate(side, j):
        for half in range(CORES):
            g = acc_g[side, j, half]
            hid[side, j, half] = (g / (1.0 + jnp.exp(-g)) * acc_u[side, j, half]).astype(
                jnp.bfloat16
            )

    def down(side, j, k):
        total = jnp.dot(
            hid[side, j, 0], wd[0, :, lanes(k)], preferred_element_type=jnp.float32
        )
        for half in range(1, CORES):
            total += jnp.dot(
                hid[side, j, half], wd[half, :, lanes(k)], preferred_element_type=jnp.float32
            )
        return total

    def arrivals(k, _):
        @pl.when(k < spread)
        def _():
            raw_rows(k).wait_recv()
            normed = raw_in[k]
            for i in range(1, groups):
                passed[i - 1, k] = jnp.dot(
                    pair_pickers[i], normed, preferred_element_type=jnp.float32
                ).astype(jnp.bfloat16)
                passing(i, k).start()
            there[0, k] = jnp.dot(
                pair_pickers[0], normed, preferred_element_type=jnp.float32
            ).astype(jnp.bfloat16)

        for j in range(1, groups):
            leaving(groups - j, k).wait_recv()

            @pl.when(k >= spread)
            def _():
                relay(j, k).start()

        @pl.when(k >= spread)
        def _():
            own_rows(k).wait_recv()

        for j in range(groups):
            project(0, own, j, k)
        project(1, there, 0, k)
        return 0

    lax.fori_loop(0, chunks, arrivals, 0)
    for j in range(groups):
        activate(0, j)

    activate(1, 0)

    def send_part(j, k):
        part_out[j, k] = down(1, j, k).astype(jnp.bfloat16)
        part(j, k).start()

    lax.fori_loop(0, ahead, lambda k, _: send_part(0, k) or 0, 0)

    def from_relay(k, _):
        for j in range(1, groups):
            relay(j, k).wait_recv()
            project(1, there, j, k)
        return 0

    lax.fori_loop(0, chunks, from_relay, 0)
    for j in range(1, groups):
        activate(1, j)

    def send_parts(k, _):
        for j in range(1, groups):
            send_part(j, k)

        @pl.when(k >= ahead)
        def _():
            send_part(0, k)

        return 0

    lax.fori_loop(0, chunks, send_parts, 0)

    def finish(k):
        part(0, k).wait_recv()
        mine = (down(0, 0, k) + part_in[0, k].astype(jnp.float32)).astype(jnp.bfloat16)
        moe = jnp.dot(placers[0], mine, preferred_element_type=jnp.float32)
        for i in range(1, groups):
            homeward(groups - i, k).wait_recv()
            moe += jnp.dot(placers[i], home_in[i - 1, k], preferred_element_type=jnp.float32)
        moe = moe * score_col
        final[0, k] = (fa[:, lanes(k)].astype(jnp.float32) + moe[:tok]).astype(jnp.bfloat16)
        result_a(k).start()
        final[1, k] = (fb[:, lanes(k)].astype(jnp.float32) + moe[tok:]).astype(jnp.bfloat16)
        result_b(k).start()

    def returns(k, _):
        @pl.when(k < chunks)
        def _():
            for j in range(1, groups):
                part(j, k).wait_recv()
                home_out[j - 1, k] = (down(0, j, k) + part_in[j, k].astype(jnp.float32)).astype(
                    jnp.bfloat16
                )
                homeward(j, k).start()

        @pl.when(k > 0)
        def _():
            finish(k - 1)

        return 0

    lax.fori_loop(0, chunks + 1, returns, 0)

    places().wait_send()
    for copy in send_weights():
        copy.wait_send()

    def drain(k, _):
        @pl.when(k < spread)
        def _():
            raw_rows(k).wait_send()
            for i in range(1, groups):
                passing(i, k).wait_send()

        @pl.when(k >= spread)
        def _():
            own_rows(k).wait_send()
            for i in range(1, groups):
                relay(i, k).wait_send()

        for i in range(1, groups):
            leaving(i, k).wait_send()
            homeward(i, k).wait_send()
        for j in range(groups):
            part(j, k).wait_send()
        result_a(k).wait()
        result_b(k).wait()
        return 0

    lax.fori_loop(0, chunks, drain, 0)


def on_device(
    flight_a, flight_b, routes_a, routes_b, scores_a, scores_b, norm_gain, w_gate, w_up, w_down
):
    ep_count = lax.axis_size("ep")
    section_count = lax.axis_size("section")
    groups = ep_count // ES
    tok, features = flight_a.shape[1:]
    hidden = w_gate.shape[2]
    capacity = min(tok, 9 * tok * TOPK * ES // (8 * ep_count))
    rows = -(-2 * capacity // 16) * 16
    width = chunk_width(features, 256)
    chunks = features // width
    bf16, f32 = jnp.bfloat16, jnp.float32
    others = groups - 1
    dma = pltpu.SemaphoreType.DMA
    vmem = pl.BlockSpec(memory_space=pltpu.VMEM)
    anywhere = pl.BlockSpec(memory_space=pl.ANY)
    out_a, out_b = pl.pallas_call(
        functools.partial(window_kernel, ep_count, section_count),
        out_shape=(
            pltpu.VMEM((tok, features), bf16),
            pltpu.VMEM((tok, features), bf16),
        ),
        in_specs=[vmem] * 7 + [anywhere] * 3,
        out_specs=(vmem, vmem),
        scratch_shapes=[
            pltpu.VMEM((CORES, features, hidden), bf16),
            pltpu.VMEM((CORES, features, hidden), bf16),
            pltpu.VMEM((CORES, hidden, features), bf16),
            pltpu.VMEM((groups, chunks, rows, width), bf16),
            pltpu.VMEM((groups, chunks, rows, width), bf16),
            pltpu.VMEM((others, chunks, rows, width), bf16),
            pltpu.VMEM((chunks, 2 * tok, width), bf16),
            pltpu.VMEM((chunks, 2 * tok, width), bf16),
            pltpu.VMEM((others, chunks, rows, width), bf16),
            pltpu.VMEM((1, 2 * tok), jnp.int32),
            pltpu.VMEM((1, 2 * tok), jnp.int32),
            pltpu.VMEM((PAIR, groups, CORES, rows, hidden), f32),
            pltpu.VMEM((PAIR, groups, CORES, rows, hidden), f32),
            pltpu.VMEM((PAIR, groups, CORES, rows, hidden), bf16),
            pltpu.VMEM((groups, chunks, rows, width), bf16),
            pltpu.VMEM((groups, chunks, rows, width), bf16),
            pltpu.VMEM((others, chunks, rows, width), bf16),
            pltpu.VMEM((others, chunks, rows, width), bf16),
            pltpu.VMEM((2, chunks, tok, width), bf16),
            dma((3,)),
            dma((1,)),
            dma((1,)),
            dma((3,)),
            dma((3,)),
            dma((chunks,)),
            dma((chunks,)),
            dma((others, chunks)),
            dma((others, chunks)),
            dma((others, chunks)),
            dma((others, chunks)),
            dma((groups, chunks)),
            dma((groups, chunks)),
            dma((others, chunks)),
            dma((others, chunks)),
            dma((2, chunks)),
            dma((2, chunks)),
        ],
        compiler_params=pltpu.CompilerParams(
            collective_id=0, has_side_effects=True, vmem_limit_bytes=60 * 1024 * 1024
        ),
    )(
        flight_a[0],
        flight_b[0],
        routes_a.reshape(1, tok),
        routes_b.reshape(1, tok),
        scores_a.reshape(1, tok),
        scores_b.reshape(1, tok),
        norm_gain,
        w_gate,
        w_up,
        w_down,
    )
    return (out_a[None], out_b[None])


def solution(mesh):
    placed = (
        P("section", "ep", None),
        P("section", "ep", None),
        P("section", None, "ep", None),
        P("section", None, "ep", None),
        P("section", None, "ep", None),
        P("section", None, "ep", None),
        P("section", None),
        P("section", None, "ep"),
        P("section", None, "ep"),
        P("section", "ep", None),
    )
    return jax.shard_map(
        on_device,
        mesh=mesh,
        in_specs=placed,
        out_specs=(P("section", "ep", None), P("section", "ep", None)),
        check_vma=False,
    )
```

```python
import functools

import jax
import jax.numpy as jnp
from jax import lax
from jax.experimental import pallas as pl
from jax.experimental.pallas import tpu as pltpu
from jax.sharding import PartitionSpec as P

ES = 4
TOPK = 1
CORES = 2
PAIR = ES // CORES

EPSILON = 1e-06
MESH = pl.DeviceIdType.MESH


def chunk_width(feature_width, most):
    return max(w for w in range(128, most + 1, 128) if feature_width % w == 0)


def spread_chunks(groups, chunks, rows, both):
    def longest(n):
        across = n * both + (chunks - n) * groups * rows
        between = (groups - 1) * rows * (chunks + n + 2)
        return max(across, between), n

    return min(longest(n) for n in range(chunks + 1))[1]


def window_kernel(
    ep_count,
    section_count,
    fa_whole,
    fb_whole,
    ra,
    rb,
    sa,
    sb,
    gain,
    w_gate,
    w_up,
    w_down,
    out_a,
    out_b,
    fa,
    fb,
    wg,
    wu,
    wd,
    own,
    there,
    leave,
    raw_in,
    passed,
    info_out,
    info_in,
    acc_g,
    acc_u,
    hid,
    part_out,
    part_in,
    home_out,
    home_in,
    final,
    w_sem,
    f_sem,
    p_send,
    p_recv,
    w_send,
    w_recv,
    r_send,
    r_recv,
    a_send,
    a_recv,
    b_send,
    b_recv,
    c_send,
    c_recv,
    d_send,
    d_recv,
    e_send,
    e_recv,
    z_send,
    z_recv,
):
    groups = ep_count // ES
    chunks, rows, width = own.shape[1:]
    tok = fa.shape[0]
    both = 2 * tok
    ahead = min(2, chunks)
    spread = spread_chunks(groups, chunks, rows, both)
    early = min(3, spread)
    sec = lax.axis_index("section")
    me = lax.axis_index("ep")
    group = me // ES
    pair = (me // CORES) % PAIR
    core = me % CORES

    def at(g, p, c):
        return (sec, g * ES + p * CORES + c)

    def group_at(i):
        return lax.rem(group + i, groups)

    partner = at(group, pair, 1 - core)
    across = at(group, 1 - pair, core)
    after = (lax.rem(sec + 1, section_count), me)
    before_dev = (lax.rem(sec + section_count - 1, section_count), me)

    barrier = pltpu.get_barrier_semaphore()
    peers = [partner, across, after, before_dev]
    peers += [at(group_at(i), pair, core) for i in range(1, groups)]
    for peer in peers:
        pl.semaphore_signal(barrier, inc=1, device_id=peer, device_id_type=MESH)

    flights = [
        pltpu.make_async_copy(src, dst, f_sem.at[n])
        for n, (src, dst) in enumerate(((fa_whole, fa), (fb_whole, fb)))
    ]
    for load in flights:
        load.start()
    loads = [
        pltpu.make_async_copy(src.at[0], dst.at[0], w_sem.at[n])
        for n, (src, dst) in enumerate(((w_gate, wg), (w_up, wu), (w_down, wd)))
    ]
    for load in loads:
        load.start()

    routes = jnp.concatenate([ra[...], rb[...]], axis=1)
    rel = routes - group
    rel = jnp.where(rel < 0, rel + groups, rel)
    padded = -(-groups // 8) * 8
    named = rel == lax.broadcasted_iota(jnp.int32, (padded, both), 0)
    named_f = jnp.where(named, 1.0, 0.0)
    first = lax.broadcasted_iota(jnp.int32, (both, both), 0)
    second = lax.broadcasted_iota(jnp.int32, (both, both), 1)
    earlier = jnp.where(first < second, 1.0, 0.0).astype(jnp.bfloat16)
    count = jnp.dot(named_f.astype(jnp.bfloat16), earlier, preferred_element_type=jnp.float32)
    slot = jnp.sum(count * named_f, axis=0, keepdims=True).astype(jnp.int32)
    place = rel * rows + slot
    diagonal = first == second
    def pick(places):
        return [
            jnp.where(
                places == lax.broadcasted_iota(jnp.int32, (rows, both), 0) + i * rows, 1.0, 0.0
            ).astype(jnp.bfloat16)
            for i in range(groups)
        ]

    pickers = pick(place)
    pl.semaphore_wait(barrier, len(peers))

    def remote(src, dst, send, recv, device):
        return pltpu.make_async_remote_copy(
            src_ref=src,
            dst_ref=dst,
            send_sem=send,
            recv_sem=recv,
            device_id=device,
            device_id_type=MESH,
        )

    def send_weights():
        return [
            remote(src.at[0], dst.at[1], w_send.at[n], w_recv.at[n], partner)
            for n, (src, dst) in enumerate(((w_gate, wg), (w_up, wu), (w_down, wd)))
        ]

    def own_rows(k):
        return remote(own.at[0, k], there.at[0, k], a_send.at[k], a_recv.at[k], across)

    def info():
        return remote(info_out, info_in, p_send.at[0], p_recv.at[0], across)

    def raw_rows(k):
        return [
            remote(
                src.at[:, lanes(k)],
                raw_in.at[k, pl.ds(n * tok, tok)],
                r_send.at[n, k],
                r_recv.at[n, k],
                across,
            )
            for n, src in enumerate((fa_whole, fb_whole))
        ]

    def passing(i, k):
        return remote(
            passed.at[i - 1, k],
            there.at[groups - i, k],
            c_send.at[i - 1, k],
            c_recv.at[groups - i - 1, k],
            at(group_at(i), pair, core),
        )

    def leaving(i, k):
        return remote(
            leave.at[i - 1, k],
            own.at[groups - i, k],
            b_send.at[i - 1, k],
            b_recv.at[groups - i - 1, k],
            at(group_at(i), pair, core),
        )

    def relay(j, k):
        return remote(
            own.at[j, k], there.at[j, k], c_send.at[j - 1, k], c_recv.at[j - 1, k], across
        )

    def part(j, k):
        return remote(part_out.at[j, k], part_in.at[j, k], d_send.at[j, k], d_recv.at[j, k], across)

    def homeward(j, k):
        return remote(
            home_out.at[j - 1, k],
            home_in.at[groups - j - 1, k],
            e_send.at[j - 1, k],
            e_recv.at[groups - j - 1, k],
            at(group_at(j), pair, core),
        )

    def lanes(k):
        return pl.ds(pl.multiple_of(k * width, 128), width)

    def result_a(k):
        return remote(final.at[0, k], out_a.at[:, lanes(k)], z_send.at[0, k], z_recv.at[0, k], after)

    def result_b(k):
        return remote(
            final.at[1, k], out_b.at[:, lanes(k)], z_send.at[1, k], z_recv.at[1, k], before_dev
        )

    def send_raw(k, _):
        for copy in raw_rows(k):
            copy.start()
        return 0

    lax.fori_loop(0, early, send_raw, 0)
    for copy in send_weights():
        copy.start()

    def inverse_rms(ref):
        def add(k, total):
            for n in range(width // 128):
                v = ref[:, pl.ds(pl.multiple_of(k * width + n * 128, 128), 128)].astype(
                    jnp.float32
                )
                total += v * v
            return total

        total = lax.fori_loop(0, chunks, add, jnp.zeros((tok, 128), jnp.float32))
        total = jnp.sum(total, axis=1, keepdims=True)
        return lax.rsqrt(total / (chunks * width) + EPSILON)

    flights[0].wait()
    inv_a = inverse_rms(fa)
    flights[1].wait()
    inv_b = inverse_rms(fb)
    inv = jnp.concatenate([inv_a, inv_b], axis=0)
    info_out[0:1] = place.astype(jnp.float32)
    info_out[1:2] = jnp.sum(jnp.where(diagonal, inv, 0.0), axis=0, keepdims=True)

    def dispatch(k, _):
        scale = gain[:, lanes(k)]
        na = (fa[:, lanes(k)].astype(jnp.float32) * inv_a * scale).astype(jnp.bfloat16)
        nb = (fb[:, lanes(k)].astype(jnp.float32) * inv_b * scale).astype(jnp.bfloat16)
        normed = jnp.concatenate([na, nb], axis=0)

        @pl.when(k + early < spread)
        def _():
            send_raw(k + early, 0)

        for i in range(1, groups):
            leave[i - 1, k] = jnp.dot(
                pickers[i], normed, preferred_element_type=jnp.float32
            ).astype(jnp.bfloat16)
            leaving(i, k).start()
        own[0, k] = jnp.dot(pickers[0], normed, preferred_element_type=jnp.float32).astype(
            jnp.bfloat16
        )

        @pl.when(k >= spread)
        def _():
            own_rows(k).start()

        return 0

    dispatch(0, 0)
    info().start()
    lax.fori_loop(1, chunks, dispatch, 0)
    acc_g[...] = jnp.zeros_like(acc_g)
    acc_u[...] = jnp.zeros_like(acc_u)
    place_col = jnp.sum(
        jnp.where(diagonal, place.astype(jnp.float32), 0.0), axis=1, keepdims=True
    ).astype(jnp.int32)
    scores = jnp.concatenate([sa[...], sb[...]], axis=1)
    score_col = jnp.sum(jnp.where(diagonal, scores, 0.0), axis=1, keepdims=True)
    placers = [
        jnp.where(
            place_col == lax.broadcasted_iota(jnp.int32, (both, rows), 1) + i * rows, 1.0, 0.0
        ).astype(jnp.bfloat16)
        for i in range(groups)
    ]

    for load in loads:
        load.wait()
    info().wait_recv()
    pair_pickers = pick(info_in[0:1].astype(jnp.int32))
    pair_inv = jnp.sum(jnp.where(diagonal, info_in[1:2], 0.0), axis=1, keepdims=True)
    for copy in send_weights():
        copy.wait_recv()

    def project(side, buffer, j, k):
        block = buffer[j, k]
        for half in range(CORES):
            acc_g[side, j, half] += jnp.dot(
                block, wg[half, pl.ds(pl.multiple_of(k * width, 128), width), :],
                preferred_element_type=jnp.float32,
            )
            acc_u[side, j, half] += jnp.dot(
                block, wu[half, pl.ds(pl.multiple_of(k * width, 128), width), :],
                preferred_element_type=jnp.float32,
            )

    def activate(side, j):
        for half in range(CORES):
            g = acc_g[side, j, half]
            hid[side, j, half] = (g / (1.0 + jnp.exp(-g)) * acc_u[side, j, half]).astype(
                jnp.bfloat16
            )

    def down(side, j, k):
        total = jnp.dot(
            hid[side, j, 0], wd[0, :, lanes(k)], preferred_element_type=jnp.float32
        )
        for half in range(1, CORES):
            total += jnp.dot(
                hid[side, j, half], wd[half, :, lanes(k)], preferred_element_type=jnp.float32
            )
        return total

    def arrivals(k, _):
        @pl.when(k < spread)
        def _():
            for copy in raw_rows(k):
                copy.wait_recv()
            normed = (raw_in[k].astype(jnp.float32) * pair_inv * gain[:, lanes(k)]).astype(
                jnp.bfloat16
            )
            for i in range(1, groups):
                passed[i - 1, k] = jnp.dot(
                    pair_pickers[i], normed, preferred_element_type=jnp.float32
                ).astype(jnp.bfloat16)
                passing(i, k).start()
            there[0, k] = jnp.dot(
                pair_pickers[0], normed, preferred_element_type=jnp.float32
            ).astype(jnp.bfloat16)

        for j in range(1, groups):
            leaving(groups - j, k).wait_recv()

            @pl.when(k >= spread)
            def _():
                relay(j, k).start()

        @pl.when(k >= spread)
        def _():
            own_rows(k).wait_recv()

        for j in range(groups):
            project(0, own, j, k)
        project(1, there, 0, k)
        return 0

    lax.fori_loop(0, chunks, arrivals, 0)
    for j in range(groups):
        activate(0, j)

    activate(1, 0)

    def send_part(j, k):
        part_out[j, k] = down(1, j, k).astype(jnp.bfloat16)
        part(j, k).start()

    lax.fori_loop(0, ahead, lambda k, _: send_part(0, k) or 0, 0)

    def from_relay(k, _):
        for j in range(1, groups):
            relay(j, k).wait_recv()
            project(1, there, j, k)
        return 0

    lax.fori_loop(0, chunks, from_relay, 0)
    for j in range(1, groups):
        activate(1, j)

    def send_parts(k, _):
        for j in range(1, groups):
            send_part(j, k)

        @pl.when(k >= ahead)
        def _():
            send_part(0, k)

        return 0

    lax.fori_loop(0, chunks, send_parts, 0)

    def finish(k):
        part(0, k).wait_recv()
        mine = (down(0, 0, k) + part_in[0, k].astype(jnp.float32)).astype(jnp.bfloat16)
        moe = jnp.dot(placers[0], mine, preferred_element_type=jnp.float32)
        for i in range(1, groups):
            homeward(groups - i, k).wait_recv()
            moe += jnp.dot(placers[i], home_in[i - 1, k], preferred_element_type=jnp.float32)
        moe = moe * score_col
        final[0, k] = (fa[:, lanes(k)].astype(jnp.float32) + moe[:tok]).astype(jnp.bfloat16)
        result_a(k).start()
        final[1, k] = (fb[:, lanes(k)].astype(jnp.float32) + moe[tok:]).astype(jnp.bfloat16)
        result_b(k).start()

    def returns(k, _):
        @pl.when(k < chunks)
        def _():
            for j in range(1, groups):
                part(j, k).wait_recv()
                home_out[j - 1, k] = (down(0, j, k) + part_in[j, k].astype(jnp.float32)).astype(
                    jnp.bfloat16
                )
                homeward(j, k).start()

        @pl.when(k > 0)
        def _():
            finish(k - 1)

        return 0

    lax.fori_loop(0, chunks + 1, returns, 0)

    info().wait_send()
    for copy in send_weights():
        copy.wait_send()

    def drain(k, _):
        @pl.when(k < spread)
        def _():
            for copy in raw_rows(k):
                copy.wait_send()
            for i in range(1, groups):
                passing(i, k).wait_send()

        @pl.when(k >= spread)
        def _():
            own_rows(k).wait_send()
            for i in range(1, groups):
                relay(i, k).wait_send()

        for i in range(1, groups):
            leaving(i, k).wait_send()
            homeward(i, k).wait_send()
        for j in range(groups):
            part(j, k).wait_send()
        result_a(k).wait()
        result_b(k).wait()
        return 0

    lax.fori_loop(0, chunks, drain, 0)


def on_device(
    flight_a, flight_b, routes_a, routes_b, scores_a, scores_b, norm_gain, w_gate, w_up, w_down
):
    ep_count = lax.axis_size("ep")
    section_count = lax.axis_size("section")
    groups = ep_count // ES
    tok, features = flight_a.shape[1:]
    hidden = w_gate.shape[2]
    capacity = min(tok, 9 * tok * TOPK * ES // (8 * ep_count))
    rows = -(-2 * capacity // 16) * 16
    width = chunk_width(features, 256)
    chunks = features // width
    bf16, f32 = jnp.bfloat16, jnp.float32
    others = groups - 1
    dma = pltpu.SemaphoreType.DMA
    vmem = pl.BlockSpec(memory_space=pltpu.VMEM)
    anywhere = pl.BlockSpec(memory_space=pl.ANY)
    out_a, out_b = pl.pallas_call(
        functools.partial(window_kernel, ep_count, section_count),
        out_shape=(
            pltpu.VMEM((tok, features), bf16),
            pltpu.VMEM((tok, features), bf16),
        ),
        in_specs=[anywhere] * 2 + [vmem] * 5 + [anywhere] * 3,
        out_specs=(vmem, vmem),
        scratch_shapes=[
            pltpu.VMEM((tok, features), bf16),
            pltpu.VMEM((tok, features), bf16),
            pltpu.VMEM((CORES, features, hidden), bf16),
            pltpu.VMEM((CORES, features, hidden), bf16),
            pltpu.VMEM((CORES, hidden, features), bf16),
            pltpu.VMEM((groups, chunks, rows, width), bf16),
            pltpu.VMEM((groups, chunks, rows, width), bf16),
            pltpu.VMEM((others, chunks, rows, width), bf16),
            pltpu.VMEM((chunks, 2 * tok, width), bf16),
            pltpu.VMEM((others, chunks, rows, width), bf16),
            pltpu.VMEM((2, 2 * tok), f32),
            pltpu.VMEM((2, 2 * tok), f32),
            pltpu.VMEM((PAIR, groups, CORES, rows, hidden), f32),
            pltpu.VMEM((PAIR, groups, CORES, rows, hidden), f32),
            pltpu.VMEM((PAIR, groups, CORES, rows, hidden), bf16),
            pltpu.VMEM((groups, chunks, rows, width), bf16),
            pltpu.VMEM((groups, chunks, rows, width), bf16),
            pltpu.VMEM((others, chunks, rows, width), bf16),
            pltpu.VMEM((others, chunks, rows, width), bf16),
            pltpu.VMEM((2, chunks, tok, width), bf16),
            dma((3,)),
            dma((2,)),
            dma((1,)),
            dma((1,)),
            dma((3,)),
            dma((3,)),
            dma((2, chunks)),
            dma((2, chunks)),
            dma((chunks,)),
            dma((chunks,)),
            dma((others, chunks)),
            dma((others, chunks)),
            dma((others, chunks)),
            dma((others, chunks)),
            dma((groups, chunks)),
            dma((groups, chunks)),
            dma((others, chunks)),
            dma((others, chunks)),
            dma((2, chunks)),
            dma((2, chunks)),
        ],
        compiler_params=pltpu.CompilerParams(
            collective_id=0, has_side_effects=True, vmem_limit_bytes=60 * 1024 * 1024
        ),
    )(
        flight_a[0],
        flight_b[0],
        routes_a.reshape(1, tok),
        routes_b.reshape(1, tok),
        scores_a.reshape(1, tok),
        scores_b.reshape(1, tok),
        norm_gain,
        w_gate,
        w_up,
        w_down,
    )
    return (out_a[None], out_b[None])


def solution(mesh):
    placed = (
        P("section", "ep", None),
        P("section", "ep", None),
        P("section", None, "ep", None),
        P("section", None, "ep", None),
        P("section", None, "ep", None),
        P("section", None, "ep", None),
        P("section", None),
        P("section", None, "ep"),
        P("section", None, "ep"),
        P("section", "ep", None),
    )
    return jax.shard_map(
        on_device,
        mesh=mesh,
        in_specs=placed,
        out_specs=(P("section", "ep", None), P("section", "ep", None)),
        check_vma=False,
    )
```

```python
import functools

import jax
import jax.numpy as jnp
from jax import lax
from jax.experimental import pallas as pl
from jax.experimental.pallas import tpu as pltpu
from jax.sharding import PartitionSpec as P

ES = 4
TOPK = 1
CORES = 2
PAIR = ES // CORES

EPSILON = 1e-06
MESH = pl.DeviceIdType.MESH


def chunk_width(feature_width, most):
    return max(w for w in range(128, most + 1, 128) if feature_width % w == 0)


def spread_chunks(groups, chunks, rows, both):
    def longest(n):
        across = n * both + (chunks - n) * groups * rows
        between = (groups - 1) * rows * (chunks + n + 2)
        return max(across, between), n

    return min(longest(n) for n in range(chunks + 1))[1]


def window_kernel(
    ep_count,
    section_count,
    fa_whole,
    fb_whole,
    ra,
    rb,
    sa,
    sb,
    gain,
    w_gate,
    w_up,
    w_down,
    out_a,
    out_b,
    fa,
    fb,
    wg,
    wu,
    wd,
    own,
    there,
    leave,
    raw_in,
    passed,
    info_out,
    info_in,
    acc_g,
    acc_u,
    hid,
    part_out,
    part_in,
    home_out,
    home_in,
    cross_out,
    cross_in,
    merged_out,
    merged_in,
    final,
    w_sem,
    f_sem,
    p_send,
    p_recv,
    w_send,
    w_recv,
    r_send,
    r_recv,
    a_send,
    a_recv,
    b_send,
    b_recv,
    c_send,
    c_recv,
    d_send,
    d_recv,
    e_send,
    e_recv,
    x_send,
    x_recv,
    m_send,
    m_recv,
    z_send,
    z_recv,
):
    groups = ep_count // ES
    chunks, rows, width = own.shape[1:]
    tok = fa.shape[0]
    both = 2 * tok
    spread = spread_chunks(groups, chunks, rows, both)
    early = min(3, spread)
    direct = chunks - spread
    ahead = min(2, direct)
    lead = min(direct + 1, chunks)
    lag = 2
    sec = lax.axis_index("section")
    me = lax.axis_index("ep")
    group = me // ES
    pair = (me // CORES) % PAIR
    core = me % CORES

    def at(g, p, c):
        return (sec, g * ES + p * CORES + c)

    def group_at(i):
        return lax.rem(group + i, groups)

    partner = at(group, pair, 1 - core)
    across = at(group, 1 - pair, core)
    after = (lax.rem(sec + 1, section_count), me)
    before_dev = (lax.rem(sec + section_count - 1, section_count), me)

    barrier = pltpu.get_barrier_semaphore()
    peers = [partner, across, after, before_dev]
    peers += [at(group_at(i), pair, core) for i in range(1, groups)]
    for peer in peers:
        pl.semaphore_signal(barrier, inc=1, device_id=peer, device_id_type=MESH)

    flights = [
        pltpu.make_async_copy(src, dst, f_sem.at[n])
        for n, (src, dst) in enumerate(((fa_whole, fa), (fb_whole, fb)))
    ]
    for load in flights:
        load.start()
    loads = [
        pltpu.make_async_copy(src.at[0], dst.at[0], w_sem.at[n])
        for n, (src, dst) in enumerate(((w_gate, wg), (w_up, wu), (w_down, wd)))
    ]
    for load in loads:
        load.start()

    routes = jnp.concatenate([ra[...], rb[...]], axis=1)
    rel = routes - group
    rel = jnp.where(rel < 0, rel + groups, rel)
    padded = -(-groups // 8) * 8
    named = rel == lax.broadcasted_iota(jnp.int32, (padded, both), 0)
    named_f = jnp.where(named, 1.0, 0.0)
    first = lax.broadcasted_iota(jnp.int32, (both, both), 0)
    second = lax.broadcasted_iota(jnp.int32, (both, both), 1)
    earlier = jnp.where(first < second, 1.0, 0.0).astype(jnp.bfloat16)
    count = jnp.dot(named_f.astype(jnp.bfloat16), earlier, preferred_element_type=jnp.float32)
    slot = jnp.sum(count * named_f, axis=0, keepdims=True).astype(jnp.int32)
    place = rel * rows + slot
    diagonal = first == second
    def pick(places):
        return [
            jnp.where(
                places == lax.broadcasted_iota(jnp.int32, (rows, both), 0) + i * rows, 1.0, 0.0
            ).astype(jnp.bfloat16)
            for i in range(groups)
        ]

    pickers = pick(place)
    pl.semaphore_wait(barrier, len(peers))

    def remote(src, dst, send, recv, device):
        return pltpu.make_async_remote_copy(
            src_ref=src,
            dst_ref=dst,
            send_sem=send,
            recv_sem=recv,
            device_id=device,
            device_id_type=MESH,
        )

    def send_weights():
        return [
            remote(src.at[0], dst.at[1], w_send.at[n], w_recv.at[n], partner)
            for n, (src, dst) in enumerate(((w_gate, wg), (w_up, wu), (w_down, wd)))
        ]

    def own_rows(k):
        return remote(own.at[0, k], there.at[0, k], a_send.at[k], a_recv.at[k], across)

    def info():
        return remote(info_out, info_in, p_send.at[0], p_recv.at[0], across)

    def raw_rows(k):
        return [
            remote(
                src.at[:, lanes(k)],
                raw_in.at[k, pl.ds(n * tok, tok)],
                r_send.at[n, k],
                r_recv.at[n, k],
                across,
            )
            for n, src in enumerate((fa_whole, fb_whole))
        ]

    def passing(i, k):
        return remote(
            passed.at[i - 1, k],
            there.at[groups - i, k],
            c_send.at[i - 1, k],
            c_recv.at[groups - i - 1, k],
            at(group_at(i), pair, core),
        )

    def leaving(i, k):
        return remote(
            leave.at[i - 1, k],
            own.at[groups - i, k],
            b_send.at[i - 1, k],
            b_recv.at[groups - i - 1, k],
            at(group_at(i), pair, core),
        )

    def relay(j, k):
        return remote(
            own.at[j, k], there.at[j, k], c_send.at[j - 1, k], c_recv.at[j - 1, k], across
        )

    def part(j, k):
        return remote(part_out.at[j, k], part_in.at[j, k], d_send.at[j, k], d_recv.at[j, k], across)

    def homeward(j, k):
        return remote(
            home_out.at[j - 1, k],
            home_in.at[groups - j - 1, k],
            e_send.at[j - 1, k],
            e_recv.at[groups - j - 1, k],
            at(group_at(j), pair, core),
        )

    def lanes(k):
        return pl.ds(pl.multiple_of(k * width, 128), width)

    def cross(j, k):
        return remote(
            cross_out.at[j - 1, k],
            cross_in.at[groups - j - 1, k],
            x_send.at[j - 1, k],
            x_recv.at[groups - j - 1, k],
            at(group_at(j), pair, core),
        )

    def merged(k):
        return remote(merged_out.at[k], merged_in.at[k], m_send.at[k], m_recv.at[k], across)

    def result_a(k):
        return remote(final.at[0, k], out_a.at[:, lanes(k)], z_send.at[0, k], z_recv.at[0, k], after)

    def result_b(k):
        return remote(
            final.at[1, k], out_b.at[:, lanes(k)], z_send.at[1, k], z_recv.at[1, k], before_dev
        )

    def send_raw(k, _):
        for copy in raw_rows(k):
            copy.start()
        return 0

    lax.fori_loop(0, early, send_raw, 0)
    for copy in send_weights():
        copy.start()

    def inverse_rms(ref):
        def add(k, total):
            for n in range(width // 128):
                v = ref[:, pl.ds(pl.multiple_of(k * width + n * 128, 128), 128)].astype(
                    jnp.float32
                )
                total += v * v
            return total

        total = lax.fori_loop(0, chunks, add, jnp.zeros((tok, 128), jnp.float32))
        total = jnp.sum(total, axis=1, keepdims=True)
        return lax.rsqrt(total / (chunks * width) + EPSILON)

    flights[0].wait()
    inv_a = inverse_rms(fa)
    flights[1].wait()
    inv_b = inverse_rms(fb)
    inv = jnp.concatenate([inv_a, inv_b], axis=0)
    info_out[0:1] = place.astype(jnp.float32)
    info_out[1:2] = jnp.sum(jnp.where(diagonal, inv, 0.0), axis=0, keepdims=True)

    def dispatch(k, _):
        scale = gain[:, lanes(k)]
        na = (fa[:, lanes(k)].astype(jnp.float32) * inv_a * scale).astype(jnp.bfloat16)
        nb = (fb[:, lanes(k)].astype(jnp.float32) * inv_b * scale).astype(jnp.bfloat16)
        normed = jnp.concatenate([na, nb], axis=0)

        @pl.when(k + early < spread)
        def _():
            send_raw(k + early, 0)

        for i in range(1, groups):
            leave[i - 1, k] = jnp.dot(
                pickers[i], normed, preferred_element_type=jnp.float32
            ).astype(jnp.bfloat16)
            leaving(i, k).start()
        own[0, k] = jnp.dot(pickers[0], normed, preferred_element_type=jnp.float32).astype(
            jnp.bfloat16
        )

        @pl.when(k >= spread)
        def _():
            own_rows(k).start()

        return 0

    dispatch(0, 0)
    info().start()
    lax.fori_loop(1, chunks, dispatch, 0)
    acc_g[...] = jnp.zeros_like(acc_g)
    acc_u[...] = jnp.zeros_like(acc_u)
    place_col = jnp.sum(
        jnp.where(diagonal, place.astype(jnp.float32), 0.0), axis=1, keepdims=True
    ).astype(jnp.int32)
    scores = jnp.concatenate([sa[...], sb[...]], axis=1)
    score_col = jnp.sum(jnp.where(diagonal, scores, 0.0), axis=1, keepdims=True)
    def spot(places_col):
        return [
            jnp.where(
                places_col == lax.broadcasted_iota(jnp.int32, (both, rows), 1) + i * rows, 1.0, 0.0
            ).astype(jnp.bfloat16)
            for i in range(groups)
        ]

    placers = spot(place_col)
    for load in loads:
        load.wait()
    info().wait_recv()
    pair_pickers = pick(info_in[0:1].astype(jnp.int32))
    pair_placers = spot(
        jnp.sum(jnp.where(diagonal, info_in[0:1], 0.0), axis=1, keepdims=True).astype(jnp.int32)
    )
    pair_inv = jnp.sum(jnp.where(diagonal, info_in[1:2], 0.0), axis=1, keepdims=True)
    for copy in send_weights():
        copy.wait_recv()

    def project(side, buffer, j, k):
        block = buffer[j, k]
        for half in range(CORES):
            acc_g[side, j, half] += jnp.dot(
                block, wg[half, pl.ds(pl.multiple_of(k * width, 128), width), :],
                preferred_element_type=jnp.float32,
            )
            acc_u[side, j, half] += jnp.dot(
                block, wu[half, pl.ds(pl.multiple_of(k * width, 128), width), :],
                preferred_element_type=jnp.float32,
            )

    def activate(side, j):
        for half in range(CORES):
            g = acc_g[side, j, half]
            hid[side, j, half] = (g / (1.0 + jnp.exp(-g)) * acc_u[side, j, half]).astype(
                jnp.bfloat16
            )

    def down(side, j, k):
        total = jnp.dot(
            hid[side, j, 0], wd[0, :, lanes(k)], preferred_element_type=jnp.float32
        )
        for half in range(1, CORES):
            total += jnp.dot(
                hid[side, j, half], wd[half, :, lanes(k)], preferred_element_type=jnp.float32
            )
        return total

    def arrivals(k, _):
        @pl.when(k < spread)
        def _():
            for copy in raw_rows(k):
                copy.wait_recv()
            normed = (raw_in[k].astype(jnp.float32) * pair_inv * gain[:, lanes(k)]).astype(
                jnp.bfloat16
            )
            for i in range(1, groups):
                passed[i - 1, k] = jnp.dot(
                    pair_pickers[i], normed, preferred_element_type=jnp.float32
                ).astype(jnp.bfloat16)
                passing(i, k).start()
            there[0, k] = jnp.dot(
                pair_pickers[0], normed, preferred_element_type=jnp.float32
            ).astype(jnp.bfloat16)

        for j in range(1, groups):
            leaving(groups - j, k).wait_recv()

            @pl.when(k >= spread)
            def _():
                relay(j, k).start()

        @pl.when(k >= spread)
        def _():
            own_rows(k).wait_recv()

        for j in range(groups):
            project(0, own, j, k)
        project(1, there, 0, k)
        return 0

    lax.fori_loop(0, chunks, arrivals, 0)
    for j in range(groups):
        activate(0, j)

    activate(1, 0)

    def send_part(j, k):
        part_out[j, k] = down(1, j, k).astype(jnp.bfloat16)
        part(j, k).start()

    def send_home(j, k):
        home_out[j - 1, k] = down(0, j, k).astype(jnp.bfloat16)
        homeward(j, k).start()

    def send_cross(j, k):
        cross_out[j - 1, k] = down(1, j, k).astype(jnp.bfloat16)
        cross(j, k).start()

    for k in range(direct, lead):
        for j in range(1, groups):
            send_home(j, k)
    lax.fori_loop(0, ahead, lambda k, _: send_part(0, k) or 0, 0)

    def from_relay(k, _):
        for j in range(1, groups):
            relay(j, k).wait_recv()
            project(1, there, j, k)
        return 0

    lax.fori_loop(0, chunks, from_relay, 0)
    for j in range(1, groups):
        activate(1, j)

    def send_parts(k, _):
        for j in range(1, groups):
            send_part(j, k)

        @pl.when(k >= ahead)
        def _():
            send_part(0, k)

        return 0

    for k in range(direct, lead):
        for j in range(1, groups):
            send_cross(j, k)
    lax.fori_loop(0, direct, send_parts, 0)

    def finish(k, split):
        mine = down(0, 0, k)
        if not split:
            part(0, k).wait_recv()
            mine += part_in[0, k].astype(jnp.float32)
        moe = jnp.dot(placers[0], mine.astype(jnp.bfloat16), preferred_element_type=jnp.float32)
        for i in range(1, groups):
            homeward(groups - i, k).wait_recv()
            moe += jnp.dot(placers[i], home_in[i - 1, k], preferred_element_type=jnp.float32)
        if split:
            merged(k).wait_recv()
            moe += merged_in[k].astype(jnp.float32)
        moe = moe * score_col
        final[0, k] = (fa[:, lanes(k)].astype(jnp.float32) + moe[:tok]).astype(jnp.bfloat16)
        result_a(k).start()
        final[1, k] = (fb[:, lanes(k)].astype(jnp.float32) + moe[tok:]).astype(jnp.bfloat16)
        result_b(k).start()

    def merge(k):
        total = jnp.dot(
            pair_placers[0], down(1, 0, k).astype(jnp.bfloat16), preferred_element_type=jnp.float32
        )
        for i in range(1, groups):
            cross(groups - i, k).wait_recv()
            total += jnp.dot(
                pair_placers[i], cross_in[i - 1, k], preferred_element_type=jnp.float32
            )
        merged_out[k] = total.astype(jnp.bfloat16)
        merged(k).start()

    def returns(k, _):
        @pl.when(k + lead < chunks)
        def _():
            for j in range(1, groups):
                send_home(j, k + lead)
                send_cross(j, k + lead)

        @pl.when(k < direct)
        def _():
            for j in range(1, groups):
                part(j, k).wait_recv()
                home_out[j - 1, k] = (down(0, j, k) + part_in[j, k].astype(jnp.float32)).astype(
                    jnp.bfloat16
                )
                homeward(j, k).start()

        @pl.when((k >= direct) & (k < chunks))
        def _():
            merge(k)

        @pl.when((k >= lag) & (k - lag < direct))
        def _():
            finish(k - lag, False)

        @pl.when(k - lag >= direct)
        def _():
            finish(k - lag, True)

        return 0

    lax.fori_loop(0, chunks + lag, returns, 0)

    info().wait_send()
    for copy in send_weights():
        copy.wait_send()

    def drain(k, _):
        @pl.when(k < spread)
        def _():
            for copy in raw_rows(k):
                copy.wait_send()
            for i in range(1, groups):
                passing(i, k).wait_send()

        @pl.when(k >= spread)
        def _():
            own_rows(k).wait_send()
            for i in range(1, groups):
                relay(i, k).wait_send()

        for i in range(1, groups):
            leaving(i, k).wait_send()
            homeward(i, k).wait_send()

        @pl.when(k < direct)
        def _():
            for j in range(groups):
                part(j, k).wait_send()

        @pl.when(k >= direct)
        def _():
            for j in range(1, groups):
                cross(j, k).wait_send()
            merged(k).wait_send()

        result_a(k).wait()
        result_b(k).wait()
        return 0

    lax.fori_loop(0, chunks, drain, 0)


def on_device(
    flight_a, flight_b, routes_a, routes_b, scores_a, scores_b, norm_gain, w_gate, w_up, w_down
):
    ep_count = lax.axis_size("ep")
    section_count = lax.axis_size("section")
    groups = ep_count // ES
    tok, features = flight_a.shape[1:]
    hidden = w_gate.shape[2]
    capacity = min(tok, 9 * tok * TOPK * ES // (8 * ep_count))
    rows = -(-2 * capacity // 16) * 16
    width = chunk_width(features, 256)
    chunks = features // width
    bf16, f32 = jnp.bfloat16, jnp.float32
    others = groups - 1
    dma = pltpu.SemaphoreType.DMA
    vmem = pl.BlockSpec(memory_space=pltpu.VMEM)
    anywhere = pl.BlockSpec(memory_space=pl.ANY)
    out_a, out_b = pl.pallas_call(
        functools.partial(window_kernel, ep_count, section_count),
        out_shape=(
            pltpu.VMEM((tok, features), bf16),
            pltpu.VMEM((tok, features), bf16),
        ),
        in_specs=[anywhere] * 2 + [vmem] * 5 + [anywhere] * 3,
        out_specs=(vmem, vmem),
        scratch_shapes=[
            pltpu.VMEM((tok, features), bf16),
            pltpu.VMEM((tok, features), bf16),
            pltpu.VMEM((CORES, features, hidden), bf16),
            pltpu.VMEM((CORES, features, hidden), bf16),
            pltpu.VMEM((CORES, hidden, features), bf16),
            pltpu.VMEM((groups, chunks, rows, width), bf16),
            pltpu.VMEM((groups, chunks, rows, width), bf16),
            pltpu.VMEM((others, chunks, rows, width), bf16),
            pltpu.VMEM((chunks, 2 * tok, width), bf16),
            pltpu.VMEM((others, chunks, rows, width), bf16),
            pltpu.VMEM((2, 2 * tok), f32),
            pltpu.VMEM((2, 2 * tok), f32),
            pltpu.VMEM((PAIR, groups, CORES, rows, hidden), f32),
            pltpu.VMEM((PAIR, groups, CORES, rows, hidden), f32),
            pltpu.VMEM((PAIR, groups, CORES, rows, hidden), bf16),
            pltpu.VMEM((groups, chunks, rows, width), bf16),
            pltpu.VMEM((groups, chunks, rows, width), bf16),
            pltpu.VMEM((others, chunks, rows, width), bf16),
            pltpu.VMEM((others, chunks, rows, width), bf16),
            pltpu.VMEM((others, chunks, rows, width), bf16),
            pltpu.VMEM((others, chunks, rows, width), bf16),
            pltpu.VMEM((chunks, 2 * tok, width), bf16),
            pltpu.VMEM((chunks, 2 * tok, width), bf16),
            pltpu.VMEM((2, chunks, tok, width), bf16),
            dma((3,)),
            dma((2,)),
            dma((1,)),
            dma((1,)),
            dma((3,)),
            dma((3,)),
            dma((2, chunks)),
            dma((2, chunks)),
            dma((chunks,)),
            dma((chunks,)),
            dma((others, chunks)),
            dma((others, chunks)),
            dma((others, chunks)),
            dma((others, chunks)),
            dma((groups, chunks)),
            dma((groups, chunks)),
            dma((others, chunks)),
            dma((others, chunks)),
            dma((others, chunks)),
            dma((others, chunks)),
            dma((chunks,)),
            dma((chunks,)),
            dma((2, chunks)),
            dma((2, chunks)),
        ],
        compiler_params=pltpu.CompilerParams(
            collective_id=0, has_side_effects=True, vmem_limit_bytes=60 * 1024 * 1024
        ),
    )(
        flight_a[0],
        flight_b[0],
        routes_a.reshape(1, tok),
        routes_b.reshape(1, tok),
        scores_a.reshape(1, tok),
        scores_b.reshape(1, tok),
        norm_gain,
        w_gate,
        w_up,
        w_down,
    )
    return (out_a[None], out_b[None])


def solution(mesh):
    placed = (
        P("section", "ep", None),
        P("section", "ep", None),
        P("section", None, "ep", None),
        P("section", None, "ep", None),
        P("section", None, "ep", None),
        P("section", None, "ep", None),
        P("section", None),
        P("section", None, "ep"),
        P("section", None, "ep"),
        P("section", "ep", None),
    )
    return jax.shard_map(
        on_device,
        mesh=mesh,
        in_specs=placed,
        out_specs=(P("section", "ep", None), P("section", "ep", None)),
        check_vma=False,
    )
```
